32 devices in a mesh: group: 2 (over x), cell: 16 (over z, y, core).
Axes of the slice: x: 2, y: 2, z: 4, core: 2. Of those that a mesh axis runs over, the one named last changes fastest.
Arguments:
- cell_factor: bfloat16 [32768, 128], P(('group', 'cell')), parts along dimension 0, may hold values from -6 to 6
- sched_factor: bfloat16 [16384, 128], P('group'), parts along dimension 0, may hold values from -6 to 6
- core_matrix: float32 [256, 128], P('group'), parts along dimension 0, may hold values from -0.03125 to 0.03125
- rate_table: bfloat16 [64, 128], replicated, may hold values from 0.5 to 2
- cell_well: int32 [32768], P(('group', 'cell')), parts along dimension 0, may hold values from 0 to 63
- sched_profile: int32 [16384], P('group'), parts along dimension 0, may hold values from 0 to 127
Outputs:
- basis_cells: float32 [32768, 256], P(('group', 'cell')), parts along dimension 0
- basis_sched: float32 [16384, 256], P(('group', 'cell')), parts along dimension 0
- core_out: float32 [512, 256], P('group'), parts along dimension 0
The draws below stay inside these ranges and needn't reach their ends.
There are 2 independent parts, one for each index of `group`. The reference program is written for one: setup_inputs(seed, part) draws one part's arguments, and reference() takes and returns one part's arrays. A program takes and returns all parts, laid end to end along the dimension named above; an argument that names none is the same for every part. Nothing has to cross between parts.
All inputs are finite; a program needn't handle non-finite values.
Results may differ from the reference program's by a relative error of at most 0.02.
Values may be sent and summed in bfloat16 or wider, within the bound.
A program may use at most 128 MiB of HBM per device.

```python
import jax
import jax.numpy as jnp
from jax import lax

R = 128
P_SIZE = 128
W = 64
CELL_DEV = 1024
NS = 8192
NC = 16384


def plant(entries, own_key, least, top_value):
    longest = entries.shape.index(max(entries.shape))
    spots = []
    for shift in (0, 1):
        where = [jax.random.randint(jax.random.fold_in(own_key, axis), (), 0, length) for axis, length in enumerate(entries.shape)]
        where[longest] = (where[longest] + shift) % entries.shape[longest]
        spots.append(tuple(where))
    return entries.at[spots[0]].set(least).at[spots[1]].set(top_value)


def shard_levels(rng, dims, split, smallest, high):
    level = 1.0
    for position, shards_of in split:
        steps = jax.random.uniform(jax.random.fold_in(jax.random.fold_in(rng, 6), position), (shards_of,), jnp.float32, smallest / len(split), high / len(split))
        level = level * jnp.repeat(jnp.exp(steps), dims[position] // shards_of).reshape((-1,) + (1,) * (len(dims) - 1 - position))
    return level


def noise(rng, dims, width, bound, split=(), held_as=jnp.bfloat16):
    values = width * jax.random.normal(rng, dims, jnp.float32)
    if split:
        values = values * shard_levels(rng, dims, split, -0.22, 0.18)
    return jnp.clip(values, -bound, bound).astype(held_as)


def setup_inputs(seed: int = 0, part: int = 0) -> dict:
    seeds = jax.random.split(jax.random.key(seed), 7)
    part_splits = jax.random.split(jax.random.fold_in(seeds[6], part), 7)
    return {
        "cell_factor": noise(part_splits[0], (NC, R), 1.0, 6.0, ((0, 16),)),
        "sched_factor": noise(part_splits[1], (NS, R), 1.0, 6.0),
        "core_matrix": noise(part_splits[2], (R, R), (1.0 / R), 0.03125, (), jnp.float32),
        "rate_table": jnp.clip(jax.random.uniform(seeds[3], (W, P_SIZE), jnp.float32, 0.5, 2.0), 0.5, 2.0).astype(jnp.bfloat16),
        "cell_well": plant(jax.random.randint(part_splits[4], (NC,), 0, W), jax.random.fold_in(part_splits[4], 1), 0, W - 1).astype(jnp.int32),
        "sched_profile": plant(jax.random.randint(part_splits[5], (NS,), 0, P_SIZE), jax.random.fold_in(part_splits[5], 1), 0, P_SIZE - 1).astype(jnp.int32),
    }


TIME_STEP = 0.25
PANEL_SCALE = 8.0

def local_gram(panel):
    return lax.dot_general(panel, panel, (((0,), (0,)), ((), ())), precision=lax.Precision.HIGHEST)

def orth_step(panel, gram):
    factor_low = jnp.linalg.cholesky(gram)
    return lax.linalg.triangular_solve(factor_low, panel, left_side=False, lower=True, transpose_a=True)

def orthonormal(panel):
    return orth_step(panel, local_gram(panel))

def build_tile(cell_rows, cell_wells, sched_factor, core_matrix, rate_table, prof_onehot):
    factor_mix = jnp.dot(cell_rows.astype(jnp.float32), core_matrix, precision=lax.Precision.HIGHEST).astype(jnp.bfloat16)
    rebuilt = lax.dot_general(factor_mix.astype(jnp.float32), sched_factor.astype(jnp.float32), (((1,), (1,)), ((), ())), preferred_element_type=jnp.float32)
    cell_rates = rate_table[cell_wells]
    inject = lax.dot_general(cell_rates.astype(jnp.float32), prof_onehot.astype(jnp.float32), (((1,), (1,)), ((), ())), preferred_element_type=jnp.float32)
    return (rebuilt + TIME_STEP * (rebuilt - rebuilt * rebuilt * rebuilt + inject)).astype(jnp.bfloat16)

def reference(cell_factor, sched_factor, core_matrix, rate_table, cell_well, sched_profile):
    n_cells = cell_factor.shape[0]
    n_sched = sched_factor.shape[0]
    widths = cell_factor.shape[1]
    blocks = n_cells // CELL_DEV
    profiles = rate_table.shape[1]
    prof_onehot = (sched_profile[:, None] == jnp.arange(profiles, dtype=jnp.int32)[None, :]).astype(jnp.bfloat16)
    factor_blocks = cell_factor.reshape(blocks, CELL_DEV, widths)
    well_blocks = cell_well.reshape(blocks, CELL_DEV)

    def first(carry, inputs):
        cell_rows, cell_wells = inputs
        tile_state = build_tile(cell_rows, cell_wells, sched_factor, core_matrix, rate_table, prof_onehot)
        k_part = jnp.dot(tile_state.astype(jnp.float32), sched_factor.astype(jnp.float32), preferred_element_type=jnp.float32)
        l_part = lax.dot_general(tile_state.astype(jnp.float32), cell_rows.astype(jnp.float32), (((0,), (0,)), ((), ())), preferred_element_type=jnp.float32)
        return (carry + l_part, k_part)
    l_proj, k_parts = lax.scan(first, jnp.zeros((n_sched, widths), jnp.float32), (factor_blocks, well_blocks))
    k_proj = k_parts.reshape(n_cells, widths)
    panel_u = jnp.concatenate([cell_factor.astype(jnp.float32), k_proj * (PANEL_SCALE / n_sched)], axis=1)
    panel_v = jnp.concatenate([sched_factor.astype(jnp.float32), l_proj * (PANEL_SCALE / n_cells)], axis=1)
    basis_u = orthonormal(panel_u)
    basis_v = orthonormal(panel_v)
    basis_low = basis_v.astype(jnp.bfloat16)
    basis_blocks = basis_u.reshape(blocks, CELL_DEV, 2 * widths)

    def second(carry, inputs):
        cell_rows, cell_wells, basis_rows = inputs
        tile_state = build_tile(cell_rows, cell_wells, sched_factor, core_matrix, rate_table, prof_onehot)
        galerkin = jnp.dot(tile_state.astype(jnp.float32), basis_low.astype(jnp.float32), preferred_element_type=jnp.float32)
        term = lax.dot_general(basis_rows, galerkin, (((0,), (0,)), ((), ())), precision=lax.Precision.HIGHEST)
        return (carry + term, 0)
    core_sum, unused = lax.scan(second, jnp.zeros((2 * widths, 2 * widths), jnp.float32), (factor_blocks, well_blocks, basis_blocks))
    basis_cells = basis_u * jnp.sqrt(jnp.float32(n_cells))
    basis_sched = basis_v * jnp.sqrt(jnp.float32(n_sched))
    core_out = core_sum * (widths / jnp.sqrt(jnp.float32(n_cells) * jnp.float32(n_sched)))
    return (basis_cells, basis_sched, core_out)
```

```python
import functools

import jax
import jax.numpy as jnp
from jax import lax
from jax.experimental import pallas as pl
from jax.experimental.pallas import tpu as pltpu
from jax.sharding import PartitionSpec as P

TIME_STEP = 0.25
PANEL_SCALE = 8.0
HIGH = lax.Precision.HIGHEST
F32 = jnp.float32
BF16 = jnp.bfloat16
CHUNKS = 4
VMEM_LIMIT = 64 * 1000 * 1000


def dot(a, b, ca, cb, precision=None):
    return lax.dot_general(
        a, b, (((ca,), (cb,)), ((), ())), precision=precision, preferred_element_type=F32
    )


def bit_order(devices):
    bits = devices.bit_length() - 1
    return [b for b in (0, 1) if b < bits] + list(range(bits - 1, 1, -1))


def owner_of(place, devices):
    order = bit_order(devices)
    bits = len(order)
    total = 0
    for s, b in enumerate(order):
        total = total + ((place // (1 << (bits - 1 - s))) % 2) * (1 << b)
    return total


def tile_kernel(
    devices, k_scale,
    cell_ref, core_ref, rate_ref, well_ref, sched_ref, prof_ref,
    ly_ref, k_ref, gram_u_ref, gram_s_ref,
    tile, mix, rates, kacc, panel_t,
):
    step = pl.program_id(0)
    cells, width = cell_ref.shape
    block = sched_ref.shape[0]
    wells, profiles = rate_ref.shape

    @pl.when(step == 0)
    def _():
        mix[...] = dot(cell_ref[...].astype(F32), core_ref[...], 1, 0, HIGH).astype(BF16)
        hot = (lax.broadcasted_iota(jnp.int32, (wells, cells), 0) == well_ref[...]).astype(F32)
        picked = dot(hot.T.astype(BF16), rate_ref[...], 1, 0)
        rates[...] = (TIME_STEP * picked).astype(BF16)
        kacc[...] = jnp.zeros_like(kacc)
        gram_s_ref[...] = jnp.zeros_like(gram_s_ref)

    @pl.when(step < devices)
    def _():
        sched = sched_ref[...]
        rebuilt = dot(mix[...], sched, 1, 1)
        hot = (
            lax.broadcasted_iota(jnp.int32, (profiles, block), 0) == prof_ref[0]
        ).astype(F32).astype(BF16)
        inject = dot(rates[...], hot, 1, 0)
        state = (
            rebuilt * ((1.0 + TIME_STEP) - TIME_STEP * (rebuilt * rebuilt)) + inject
        ).astype(BF16)
        tile[step] = state
        kacc[...] += dot(state, sched, 1, 0)
        gram_s_ref[...] += dot(sched.astype(F32).T.astype(BF16), sched, 1, 0)

    @pl.when(step == devices - 1)
    def _():
        k = kacc[...] * k_scale
        k_ref[...] = k
        k_t = k.T
        cell_t = cell_ref[...].astype(F32).T
        both = jnp.concatenate([cell_t, k_t], axis=0)
        panel_t[...] = both.astype(BF16)
        gram_u_ref[...] = dot(both, both, 1, 1, HIGH)

    @pl.when(step >= devices)
    def _():
        owner = owner_of(step - devices, devices)
        ly_ref[0] = dot(panel_t[...], tile[owner], 1, 0).astype(BF16)


def comm_kernel(
    devices, l_scale,
    x_ref, gram_ref,
    ly_ref, gram_out, lg_out,
    *scratch,
):
    order = bit_order(devices)
    stages = len(order)
    recv = scratch[:stages]
    g_recv, g_acc, l_recv, l_acc, xs, xr, gs, gr, ls, lr = scratch[stages:]
    me = lax.axis_index("cell")
    rows = x_ref.shape[1] // CHUNKS
    digits = [(me // (1 << b)) % 2 for b in order]
    partners = [me + (1 - 2 * d) * (1 << b) for d, b in zip(digits, order)]

    barrier = pltpu.get_barrier_semaphore()
    for p in partners:
        pl.semaphore_signal(
            barrier, inc=1, device_id={"cell": p}, device_id_type=pl.DeviceIdType.MESH
        )
    pl.semaphore_wait(barrier, stages)

    def remote(src, dst, ssem, rsem, s):
        return pltpu.make_async_remote_copy(
            src_ref=src, dst_ref=dst, send_sem=ssem, recv_sem=rsem,
            device_id={"cell": partners[s]}, device_id_type=pl.DeviceIdType.MESH,
        )

    def big(s, c):
        half = devices >> (s + 1)
        cur = x_ref if s == 0 else recv[s - 1]
        part = pl.ds(c * rows, rows)
        return remote(
            cur.at[pl.ds((1 - digits[s]) * half, half), part],
            recv[s].at[:, part], xs.at[s, c], xr.at[s, c], s,
        )

    def small(s, buf, acc, ssem, rsem):
        return remote(acc.at[s], buf.at[s], ssem.at[s], rsem.at[s], s)

    def fold(s, c):
        half = devices >> (s + 1)
        cur = x_ref if s == 0 else recv[s - 1]
        part = pl.ds(c * rows, rows)
        if s == stages - 1:
            ly_ref[part] = (
                recv[s][0, part].astype(F32) + cur[digits[s], part].astype(F32)
            )
        else:
            def body(i, carry):
                recv[s][i, part] = (
                    recv[s][i, part].astype(F32)
                    + cur[digits[s] * half + i, part].astype(F32)
                ).astype(BF16)
                return carry
            lax.fori_loop(0, half, body, 0)

    g_acc[0] = gram_ref[...]
    small(0, g_recv, g_acc, gs, gr).start()
    for c in range(CHUNKS):
        big(0, c).start()
    for d in range(stages + CHUNKS - 1):
        for s in range(stages - 1, -1, -1):
            c = d - s
            if 0 <= c < CHUNKS:
                big(s, c).wait_recv()
                fold(s, c)
                if s + 1 < stages:
                    big(s + 1, c).start()
        if d < stages:
            small(d, g_recv, g_acc, gs, gr).wait_recv()
            total = g_acc[d] + g_recv[d]
            if d + 1 < stages:
                g_acc[d + 1] = total
                small(d + 1, g_recv, g_acc, gs, gr).start()
            else:
                gram_out[...] = total
    width = l_acc.shape[2]
    left = ly_ref[0:width]
    l_acc[0] = dot(ly_ref[...], left, 1, 1, HIGH)
    for s in range(stages):
        copy = small(s, l_recv, l_acc, ls, lr)
        copy.start()
        copy.wait_recv()
        total = l_acc[s] + l_recv[s]
        if s + 1 < stages:
            l_acc[s + 1] = total
        else:
            lg_out[...] = total
    for s in range(stages):
        for c in range(CHUNKS):
            big(s, c).wait_send()
        small(s, g_recv, g_acc, gs, gr).wait_send()
        small(s, l_recv, l_acc, ls, lr).wait_send()


def eliminate(w, pieces=4):
    n = w.shape[1]
    size = n // pieces
    for piece in range(pieces):
        low = piece * size
        count = n - low
        row_id = lax.broadcasted_iota(jnp.int32, (count, 1), 0) + low
        lane_id = lax.broadcasted_iota(jnp.int32, (1, n), 1)

        def body(t, carry):
            j = low + t
            here = lane_id == j
            for m in range(2):
                row = w[m, pl.ds(j, 1), :]
                col = jnp.sum(
                    jnp.where(here, w[m, low:n, 0:n], 0.0), axis=1, keepdims=True
                )
                pivot = jnp.sum(jnp.where(here, row[:, 0:n], 0.0), axis=1, keepdims=True)
                factor = jnp.where(row_id > j, col * (1.0 / pivot), 0.0)
                w[m, low:n, :] = w[m, low:n, :] - factor * row
            return carry

        lax.fori_loop(0, size, body, 0)


def inverse_pair(w, first, second):
    n = w.shape[1]
    eye = (
        lax.broadcasted_iota(jnp.int32, (n, n), 0) == lax.broadcasted_iota(jnp.int32, (n, n), 1)
    ).astype(F32)
    for m, a in enumerate((first, second)):
        w[m, :, 0:n] = a
        w[m, :, n : 2 * n] = eye
    eliminate(w)
    outs = []
    for m in range(2):
        diag = jnp.sum(w[m, :, 0:n] * eye, axis=1, keepdims=True)
        outs.append(w[m, :, n : 2 * n] * lax.rsqrt(diag))
    return outs


def finish_kernel(
    n_cells, n_sched, l_scale,
    gram_u_ref, gram_s_ref, lg_ref, cell_ref, k_ref, sched_ref, ly_ref,
    cells_ref, rows_ref, core_ref,
    w,
):
    n = gram_s_ref.shape[0]
    cc, ck, kk = gram_u_ref[0:n, 0:n], gram_u_ref[0:n, n:], gram_u_ref[n:, n:]
    sl = (ck.T) * (n_sched / n_cells)
    ll = lg_ref[0:n] * (l_scale * l_scale)
    yl = lg_ref[n:] * l_scale
    u11, v11 = inverse_pair(w, cc, gram_s_ref[...])
    xu = dot(u11, ck, 1, 0, HIGH)
    xv = dot(v11, sl, 1, 0, HIGH)
    u22, v22 = inverse_pair(w, kk - dot(xu.T, xu, 1, 0, HIGH), ll - dot(xv.T, xv, 1, 0, HIGH))
    u21 = -dot(u22, dot(xu.T, u11, 1, 0, HIGH), 1, 0, HIGH)
    v21 = -dot(v22, dot(xv.T, v11, 1, 0, HIGH), 1, 0, HIGH)

    size_u = float(n_cells) ** 0.5
    size_v = float(n_sched) ** 0.5
    cell = cell_ref[...].astype(F32)
    cells_ref[:, 0:n] = dot(cell, u11 * size_u, 1, 1, HIGH)
    cells_ref[:, n:] = dot(cell, u21 * size_u, 1, 1, HIGH) + dot(
        k_ref[...], u22 * size_u, 1, 1, HIGH
    )
    sched = sched_ref[...].astype(F32)
    l_rows = (ly_ref[0:n] * l_scale).T
    rows_ref[:, 0:n] = dot(sched, v11 * size_v, 1, 1, HIGH)
    rows_ref[:, n:] = dot(sched, v21 * size_v, 1, 1, HIGH) + dot(
        l_rows, v22 * size_v, 1, 1, HIGH
    )

    k_unscale = n_sched / PANEL_SCALE
    l_unscale = n_cells / PANEL_SCALE
    m11 = ck * k_unscale
    m12 = ll * l_unscale
    m21 = kk * k_unscale
    m22 = yl
    t11 = dot(u11, m11, 1, 0, HIGH)
    t12 = dot(u11, m12, 1, 0, HIGH)
    t21 = dot(u21, m11, 1, 0, HIGH) + dot(u22, m21, 1, 0, HIGH)
    t22 = dot(u21, m12, 1, 0, HIGH) + dot(u22, m22, 1, 0, HIGH)
    scale = n / (float(n_cells) * float(n_sched)) ** 0.5
    core_ref[0:n, 0:n] = scale * dot(t11, v11, 1, 1, HIGH)
    core_ref[n:, 0:n] = scale * dot(t21, v11, 1, 1, HIGH)
    core_ref[0:n, n:] = scale * (dot(t11, v21, 1, 1, HIGH) + dot(t12, v22, 1, 1, HIGH))
    core_ref[n:, n:] = scale * (dot(t21, v21, 1, 1, HIGH) + dot(t22, v22, 1, 1, HIGH))


def local(cell_factor, sched_factor, core_matrix, rate_table, cell_well, sched_profile):
    cells, width = cell_factor.shape
    n_sched = sched_factor.shape[0]
    devices = lax.axis_size("cell")
    n_cells = cells * devices
    block = n_sched // devices
    wells, profiles = rate_table.shape
    stages = devices.bit_length() - 1
    l_scale = PANEL_SCALE / n_cells
    full = lambda *shape: pl.BlockSpec(shape, lambda i: (0,) * len(shape))
    sds = jax.ShapeDtypeStruct

    ly_parts, k, gram_u, gram_s = pl.pallas_call(
        functools.partial(tile_kernel, devices, PANEL_SCALE / n_sched),
        grid=(2 * devices,),
        in_specs=[
            full(cells, width),
            full(width, width),
            full(wells, profiles),
            full(1, cells),
            pl.BlockSpec((block, width), lambda i: (jnp.minimum(i, devices - 1), 0)),
            pl.BlockSpec((1, 1, block), lambda i: (jnp.minimum(i, devices - 1), 0, 0)),
        ],
        out_specs=[
            pl.BlockSpec(
                (1, 2 * width, block), lambda i: (jnp.maximum(i - devices, 0), 0, 0)
            ),
            full(cells, width),
            full(2 * width, 2 * width),
            full(width, width),
        ],
        out_shape=[
            sds((devices, 2 * width, block), BF16),
            sds((cells, width), F32),
            sds((2 * width, 2 * width), F32),
            sds((width, width), F32),
        ],
        scratch_shapes=[
            pltpu.VMEM((devices, cells, block), BF16),
            pltpu.VMEM((cells, width), BF16),
            pltpu.VMEM((cells, profiles), BF16),
            pltpu.VMEM((cells, width), F32),
            pltpu.VMEM((2 * width, cells), BF16),
        ],
        compiler_params=pltpu.CompilerParams(
            dimension_semantics=("arbitrary",), vmem_limit_bytes=VMEM_LIMIT
        ),
    )(
        cell_factor, core_matrix, rate_table, cell_well.reshape(1, cells),
        sched_factor, sched_profile.reshape(devices, 1, block),
    )

    vmem = pl.BlockSpec(memory_space=pltpu.VMEM)
    dma = pltpu.SemaphoreType.DMA
    ly, gram_u, lg = pl.pallas_call(
        functools.partial(comm_kernel, devices, l_scale),
        in_specs=[vmem, vmem],
        out_specs=[vmem, vmem, vmem],
        out_shape=[
            sds((2 * width, block), F32),
            sds((2 * width, 2 * width), F32),
            sds((2 * width, width), F32),
        ],
        scratch_shapes=[
            pltpu.VMEM((devices >> (s + 1), 2 * width, block), BF16) for s in range(stages)
        ]
        + [
            pltpu.VMEM((stages, 2 * width, 2 * width), F32),
            pltpu.VMEM((stages, 2 * width, 2 * width), F32),
            pltpu.VMEM((stages, 2 * width, width), F32),
            pltpu.VMEM((stages, 2 * width, width), F32),
            dma((stages, CHUNKS)), dma((stages, CHUNKS)),
            dma((stages,)), dma((stages,)), dma((stages,)), dma((stages,)),
        ],
        compiler_params=pltpu.CompilerParams(
            collective_id=0, has_side_effects=True, vmem_limit_bytes=VMEM_LIMIT
        ),
    )(ly_parts, gram_u)

    row_start = lax.axis_index("cell") * block
    sched_rows = lax.dynamic_slice_in_dim(sched_factor, row_start, block, 0)
    return pl.pallas_call(
        functools.partial(finish_kernel, n_cells, n_sched, l_scale),
        in_specs=[vmem] * 7,
        out_specs=[vmem] * 3,
        out_shape=[
            sds((cells, 2 * width), F32),
            sds((block, 2 * width), F32),
            sds((2 * width, 2 * width), F32),
        ],
        scratch_shapes=[pltpu.VMEM((2, width, 2 * width), F32)],
        compiler_params=pltpu.CompilerParams(vmem_limit_bytes=VMEM_LIMIT),
    )(gram_u, gram_s, lg, cell_factor, k, sched_rows, ly)


def solution(mesh):
    return jax.shard_map(
        local,
        mesh=mesh,
        in_specs=(
            P(("group", "cell"), None),
            P("group", None),
            P("group", None),
            P(),
            P(("group", "cell")),
            P("group"),
        ),
        out_specs=(P(("group", "cell"), None), P(("group", "cell"), None), P("group", None)),
        check_vma=False,
    )
```

```python
import functools

import jax
import jax.numpy as jnp
from jax import lax
from jax.experimental import pallas as pl
from jax.experimental.pallas import tpu as pltpu
from jax.sharding import PartitionSpec as P

TIME_STEP = 0.25
PANEL_SCALE = 8.0
HIGH = lax.Precision.HIGHEST
F32 = jnp.float32
BF16 = jnp.bfloat16
CHUNKS = 4
BLOCK = 16
VMEM_LIMIT = 64 * 1000 * 1000


def dot(a, b, ca, cb, precision=None):
    return lax.dot_general(
        a, b, (((ca,), (cb,)), ((), ())), precision=precision, preferred_element_type=F32
    )


def bit_order(devices):
    bits = devices.bit_length() - 1
    return [b for b in (0, 1) if b < bits] + list(range(bits - 1, 1, -1))


def owner_of(place, devices):
    order = bit_order(devices)
    bits = len(order)
    total = 0
    for s, b in enumerate(order):
        total = total + ((place // (1 << (bits - 1 - s))) % 2) * (1 << b)
    return total


def tile_kernel(
    devices, k_scale,
    cell_ref, core_ref, rate_ref, well_ref, sched_ref, prof_ref,
    ly_ref, k_ref, gram_u_ref, gram_s_ref,
    tile, mix, rates, kacc, panel_t,
):
    step = pl.program_id(0)
    cells, width = cell_ref.shape
    block = sched_ref.shape[0]
    wells, profiles = rate_ref.shape

    @pl.when(step == 0)
    def _():
        mix[...] = dot(cell_ref[...].astype(F32), core_ref[...], 1, 0, HIGH).astype(BF16)
        hot = (lax.broadcasted_iota(jnp.int32, (wells, cells), 0) == well_ref[...]).astype(F32)
        picked = dot(hot.T.astype(BF16), rate_ref[...], 1, 0)
        rates[...] = (TIME_STEP * picked).astype(BF16)
        kacc[...] = jnp.zeros_like(kacc)
        gram_s_ref[...] = jnp.zeros_like(gram_s_ref)

    @pl.when(step < devices)
    def _():
        sched = sched_ref[...]
        rebuilt = dot(mix[...], sched, 1, 1)
        hot = (
            lax.broadcasted_iota(jnp.int32, (profiles, block), 0) == prof_ref[0]
        ).astype(F32).astype(BF16)
        inject = dot(rates[...], hot, 1, 0)
        state = (
            rebuilt * ((1.0 + TIME_STEP) - TIME_STEP * (rebuilt * rebuilt)) + inject
        ).astype(BF16)
        tile[step] = state
        kacc[...] += dot(state, sched, 1, 0)
        gram_s_ref[...] += dot(sched.astype(F32).T.astype(BF16), sched, 1, 0)

    @pl.when(step == devices - 1)
    def _():
        k = kacc[...] * k_scale
        k_ref[...] = k
        k_t = k.T
        cell_t = cell_ref[...].astype(F32).T
        both = jnp.concatenate([cell_t, k_t], axis=0)
        panel_t[...] = both.astype(BF16)
        gram_u_ref[...] = dot(both, both, 1, 1, HIGH)

    @pl.when(step >= devices)
    def _():
        owner = owner_of(step - devices, devices)
        ly_ref[0] = dot(panel_t[...], tile[owner], 1, 0).astype(BF16)


def eliminate(w, m, low, high):
    n = w.shape[1]
    lane = lax.broadcasted_iota(jnp.int32, (1, n), 1)
    rid = lax.broadcasted_iota(jnp.int32, (BLOCK, 1), 0)

    def body(b, carry):
        base = pl.multiple_of(b * BLOCK, BLOCK)
        rows = w[m, pl.ds(base, BLOCK), :]
        cols = [
            jnp.sum(jnp.where(lane == base + t, rows[:, 0:n], 0.0), axis=1, keepdims=True)
            for t in range(BLOCK)
        ]
        inverse = jnp.zeros((BLOCK, 1), F32)
        for t in range(BLOCK):
            recip = 1.0 / cols[t][t : t + 1, :]
            inverse = jnp.where(rid == t, recip, inverse)
            factor = jnp.where(rid > t, cols[t] * recip, 0.0)
            for later in range(t + 1, BLOCK):
                cols[later] = cols[later] - factor * cols[later][t : t + 1, :]
            rows = rows - factor * rows[t : t + 1, :]
        w[m, pl.ds(base, BLOCK), :] = rows
        left = jnp.where(lane >= base + BLOCK, rows[:, 0:n] * inverse, 0.0)
        w[m] = w[m] - dot(left, rows, 0, 0, HIGH)
        return carry

    lax.fori_loop(low, high, body, 0)


def identity(n):
    return (
        lax.broadcasted_iota(jnp.int32, (n, n), 0) == lax.broadcasted_iota(jnp.int32, (n, n), 1)
    ).astype(F32)


def load(w, m, a):
    n = w.shape[1]
    w[m, :, 0:n] = a
    w[m, :, n : 2 * n] = identity(n)


def factor_inverse(w, m):
    n = w.shape[1]
    diag = jnp.sum(w[m, :, 0:n] * identity(n), axis=1, keepdims=True)
    return w[m, :, n : 2 * n] * lax.rsqrt(diag)


def comm_kernel(
    devices, n_cells, n_sched,
    x_ref, gram_ref, gram_s_ref, cell_ref, k_ref, sched_ref,
    cells_ref, rows_ref, core_ref,
    *scratch,
):
    order = bit_order(devices)
    stages = len(order)
    recv = scratch[:stages]
    (
        ly, g_recv, g_acc, l_recv, l_acc, y_recv, y_acc, w, inv, sched_own,
        xs, xr, gs, gr, ls, lr, ys, yr, own_sem,
    ) = scratch[stages:]
    n = gram_s_ref.shape[0]
    l_scale = PANEL_SCALE / n_cells
    me = lax.axis_index("cell")
    block = sched_own.shape[0]
    rows = x_ref.shape[1] // CHUNKS
    digits = [(me // (1 << b)) % 2 for b in order]
    partners = [me + (1 - 2 * d) * (1 << b) for d, b in zip(digits, order)]

    own = pltpu.make_async_copy(
        sched_ref.at[pl.ds(pl.multiple_of(me * block, block), block)], sched_own, own_sem
    )
    own.start()
    barrier = pltpu.get_barrier_semaphore()
    for p in partners:
        pl.semaphore_signal(
            barrier, inc=1, device_id={"cell": p}, device_id_type=pl.DeviceIdType.MESH
        )
    pl.semaphore_wait(barrier, stages)

    def remote(src, dst, ssem, rsem, s):
        return pltpu.make_async_remote_copy(
            src_ref=src, dst_ref=dst, send_sem=ssem, recv_sem=rsem,
            device_id={"cell": partners[s]}, device_id_type=pl.DeviceIdType.MESH,
        )

    def big(s, c):
        half = devices >> (s + 1)
        cur = x_ref if s == 0 else recv[s - 1]
        part = pl.ds(c * rows, rows)
        return remote(
            cur.at[pl.ds((1 - digits[s]) * half, half), part],
            recv[s].at[:, part], xs.at[s, c], xr.at[s, c], s,
        )

    def fold(s, c):
        half = devices >> (s + 1)
        cur = x_ref if s == 0 else recv[s - 1]
        part = pl.ds(c * rows, rows)
        if s == stages - 1:
            ly[part] = recv[s][0, part].astype(F32) + cur[digits[s], part].astype(F32)
        else:
            def body(i, carry):
                recv[s][i, part] = (
                    recv[s][i, part].astype(F32)
                    + cur[digits[s] * half + i, part].astype(F32)
                ).astype(BF16)
                return carry
            lax.fori_loop(0, half, body, 0)

    small = {"g": (g_recv, g_acc, gs, gr), "l": (l_recv, l_acc, ls, lr), "y": (y_recv, y_acc, ys, yr)}

    def hop(name, s):
        buf, acc, ssem, rsem = small[name]
        return remote(acc.at[s], buf.at[s], ssem.at[s], rsem.at[s], s)

    def begin(name, value):
        small[name][1][0] = value
        hop(name, 0).start()

    def advance(name, s):
        buf, acc, _, _ = small[name]
        hop(name, s).wait_recv()
        acc[s + 1] = acc[s] + buf[s]
        if s + 1 < stages:
            hop(name, s + 1).start()

    begin("g", jnp.concatenate([gram_ref[0:n, 0:n], gram_ref[0:n, n:], gram_ref[n:, n:]], axis=0))
    for c in range(CHUNKS):
        big(0, c).start()

    pieces = n // BLOCK
    cut = pieces // 2
    g = lambda i: g_acc[stages, i * n : (i + 1) * n]
    size_u = float(n_cells) ** 0.5
    size_v = float(n_sched) ** 0.5

    def schur(slot, corner, side, square):
        x = dot(inv[slot], side, 1, 0, HIGH)
        inv[slot + 1] = dot(x, inv[slot], 0, 0, HIGH)
        load(w, corner, square - dot(x, x, 0, 0, HIGH))

    def work_v_first():
        load(w, 1, gram_s_ref[...])
        eliminate(w, 1, 0, cut)

    def work_v_second():
        eliminate(w, 1, cut, pieces)
        inv[3] = factor_inverse(w, 1)

    def work_u_first():
        load(w, 0, g(0))
        eliminate(w, 0, 0, pieces)
        inv[0] = factor_inverse(w, 0)

    def work_u_second():
        schur(0, 0, g(1), g(2))
        eliminate(w, 0, 0, cut)

    def work_u_third():
        eliminate(w, 0, cut, pieces)
        inv[2] = factor_inverse(w, 0)
        inv[1] = -dot(inv[2], inv[1], 1, 0, HIGH)

    def work_cells():
        cell = cell_ref[...].astype(F32)
        cells_ref[:, 0:n] = dot(cell, inv[0] * size_u, 1, 1, HIGH)
        cells_ref[:, n:] = dot(cell, inv[1] * size_u, 1, 1, HIGH) + dot(
            k_ref[...], inv[2] * size_u, 1, 1, HIGH
        )

    jobs = [work_v_first, work_v_second, work_u_first, work_u_second, work_u_third, work_cells]
    done = 0
    for d in range(stages + CHUNKS - 1):
        for s in range(stages - 1, -1, -1):
            c = d - s
            if 0 <= c < CHUNKS:
                big(s, c).wait_recv()
                fold(s, c)
                if s + 1 < stages:
                    big(s + 1, c).start()
        if d < stages:
            advance("g", d)
        if d < stages + CHUNKS - 2 and done < len(jobs) and (done < 2 or d >= stages - 1):
            jobs[done]()
            done += 1

    left = ly[0:n]
    begin("l", dot(left, left, 1, 1, HIGH))
    begin("y", dot(ly[n : 2 * n], left, 1, 1, HIGH))
    for job in jobs[done : done + 1]:
        job()
    for s in range(stages):
        advance("l", s)
        for job in jobs[done + 1 + s : done + 2 + s]:
            job()
    ll = l_acc[stages] * (l_scale * l_scale)
    ck = g(1)
    schur(3, 1, ck.T * (n_sched / n_cells), ll)
    for s in range(stages):
        advance("y", s)
        eliminate(w, 1, pieces * s // stages, pieces * (s + 1) // stages)
    inv[5] = factor_inverse(w, 1)
    inv[4] = -dot(inv[5], inv[4], 1, 0, HIGH)
    yl = y_acc[stages] * l_scale
    u11, u21, u22, v11, v21, v22 = [inv[i] for i in range(6)]

    own.wait()
    sched = sched_own[...].astype(F32)
    l_rows = (left * l_scale).T
    rows_ref[:, 0:n] = dot(sched, v11 * size_v, 1, 1, HIGH)
    rows_ref[:, n:] = dot(sched, v21 * size_v, 1, 1, HIGH) + dot(
        l_rows, v22 * size_v, 1, 1, HIGH
    )

    k_unscale = n_sched / PANEL_SCALE
    m11 = ck * k_unscale
    m12 = ll * (1.0 / l_scale)
    m21 = g(2) * k_unscale
    t11 = dot(u11, m11, 1, 0, HIGH)
    t12 = dot(u11, m12, 1, 0, HIGH)
    t21 = dot(u21, m11, 1, 0, HIGH) + dot(u22, m21, 1, 0, HIGH)
    t22 = dot(u21, m12, 1, 0, HIGH) + dot(u22, yl, 1, 0, HIGH)
    scale = n / (float(n_cells) * float(n_sched)) ** 0.5
    core_ref[0:n, 0:n] = scale * dot(t11, v11, 1, 1, HIGH)
    core_ref[n:, 0:n] = scale * dot(t21, v11, 1, 1, HIGH)
    core_ref[0:n, n:] = scale * (dot(t11, v21, 1, 1, HIGH) + dot(t12, v22, 1, 1, HIGH))
    core_ref[n:, n:] = scale * (dot(t21, v21, 1, 1, HIGH) + dot(t22, v22, 1, 1, HIGH))
    for s in range(stages):
        for c in range(CHUNKS):
            big(s, c).wait_send()
        for name in small:
            hop(name, s).wait_send()


def local(cell_factor, sched_factor, core_matrix, rate_table, cell_well, sched_profile):
    cells, width = cell_factor.shape
    n_sched = sched_factor.shape[0]
    devices = lax.axis_size("cell")
    n_cells = cells * devices
    block = n_sched // devices
    wells, profiles = rate_table.shape
    stages = devices.bit_length() - 1
    full = lambda *shape: pl.BlockSpec(shape, lambda i: (0,) * len(shape))
    sds = jax.ShapeDtypeStruct

    ly_parts, k, gram_u, gram_s = pl.pallas_call(
        functools.partial(tile_kernel, devices, PANEL_SCALE / n_sched),
        grid=(2 * devices,),
        in_specs=[
            full(cells, width),
            full(width, width),
            full(wells, profiles),
            full(1, cells),
            pl.BlockSpec((block, width), lambda i: (jnp.minimum(i, devices - 1), 0)),
            pl.BlockSpec((1, 1, block), lambda i: (jnp.minimum(i, devices - 1), 0, 0)),
        ],
        out_specs=[
            pl.BlockSpec(
                (1, 2 * width, block), lambda i: (jnp.maximum(i - devices, 0), 0, 0)
            ),
            full(cells, width),
            full(2 * width, 2 * width),
            full(width, width),
        ],
        out_shape=[
            sds((devices, 2 * width, block), BF16),
            sds((cells, width), F32),
            sds((2 * width, 2 * width), F32),
            sds((width, width), F32),
        ],
        scratch_shapes=[
            pltpu.VMEM((devices, cells, block), BF16),
            pltpu.VMEM((cells, width), BF16),
            pltpu.VMEM((cells, profiles), BF16),
            pltpu.VMEM((cells, width), F32),
            pltpu.VMEM((2 * width, cells), BF16),
        ],
        compiler_params=pltpu.CompilerParams(
            dimension_semantics=("arbitrary",), vmem_limit_bytes=VMEM_LIMIT
        ),
    )(
        cell_factor, core_matrix, rate_table, cell_well.reshape(1, cells),
        sched_factor, sched_profile.reshape(devices, 1, block),
    )

    vmem = pl.BlockSpec(memory_space=pltpu.VMEM)
    dma = pltpu.SemaphoreType.DMA
    rest = pl.BlockSpec(memory_space=pl.ANY)
    return pl.pallas_call(
        functools.partial(comm_kernel, devices, n_cells, n_sched),
        in_specs=[vmem] * 5 + [rest],
        out_specs=[vmem] * 3,
        out_shape=[
            sds((cells, 2 * width), F32),
            sds((block, 2 * width), F32),
            sds((2 * width, 2 * width), F32),
        ],
        scratch_shapes=[
            pltpu.VMEM((devices >> (s + 1), 2 * width, block), BF16) for s in range(stages)
        ]
        + [
            pltpu.VMEM((2 * width, block), F32),
            pltpu.VMEM((stages, 3 * width, width), F32),
            pltpu.VMEM((stages + 1, 3 * width, width), F32),
            pltpu.VMEM((stages, width, width), F32),
            pltpu.VMEM((stages + 1, width, width), F32),
            pltpu.VMEM((stages, width, width), F32),
            pltpu.VMEM((stages + 1, width, width), F32),
            pltpu.VMEM((2, width, 2 * width), F32),
            pltpu.VMEM((6, width, width), F32),
            pltpu.VMEM((block, width), BF16),
            dma((stages, CHUNKS)), dma((stages, CHUNKS)),
        ]
        + [dma((stages,))] * 6
        + [dma],
        compiler_params=pltpu.CompilerParams(
            collective_id=0, has_side_effects=True, vmem_limit_bytes=VMEM_LIMIT
        ),
    )(ly_parts, gram_u, gram_s, cell_factor, k, sched_factor)


def solution(mesh):
    return jax.shard_map(
        local,
        mesh=mesh,
        in_specs=(
            P(("group", "cell"), None),
            P("group", None),
            P("group", None),
            P(),
            P(("group", "cell")),
            P("group"),
        ),
        out_specs=(P(("group", "cell"), None), P(("group", "cell"), None), P("group", None)),
        check_vma=False,
    )
```

```python
import functools

import jax
import jax.numpy as jnp
from jax import lax
from jax.experimental import pallas as pl
from jax.experimental.pallas import tpu as pltpu
from jax.sharding import PartitionSpec as P

TIME_STEP = 0.25
PANEL_SCALE = 8.0
HIGH = lax.Precision.HIGHEST
F32 = jnp.float32
BF16 = jnp.bfloat16
CHUNKS = 4
BLOCK = 16
VMEM_LIMIT = 64 * 1000 * 1000


def dot(a, b, ca, cb, precision=None):
    return lax.dot_general(
        a, b, (((ca,), (cb,)), ((), ())), precision=precision, preferred_element_type=F32
    )


def bit_order(devices):
    bits = devices.bit_length() - 1
    return [b for b in (0, 1) if b < bits] + list(range(bits - 1, 1, -1))


def owner_of(place, devices):
    order = bit_order(devices)
    bits = len(order)
    total = 0
    for s, b in enumerate(order):
        total = total + ((place // (1 << (bits - 1 - s))) % 2) * (1 << b)
    return total


def eliminate(w, m, low, high):
    n = w.shape[1]
    lane = lax.broadcasted_iota(jnp.int32, (1, n), 1)
    rid = lax.broadcasted_iota(jnp.int32, (BLOCK, 1), 0)

    def body(b, carry):
        base = pl.multiple_of(b * BLOCK, BLOCK)
        rows = w[m, pl.ds(base, BLOCK), :]
        cols = [
            jnp.sum(jnp.where(lane == base + t, rows[:, 0:n], 0.0), axis=1, keepdims=True)
            for t in range(BLOCK)
        ]
        inverse = jnp.zeros((BLOCK, 1), F32)
        for t in range(BLOCK):
            recip = 1.0 / cols[t][t : t + 1, :]
            inverse = jnp.where(rid == t, recip, inverse)
            factor = jnp.where(rid > t, cols[t] * recip, 0.0)
            for later in range(t + 1, BLOCK):
                cols[later] = cols[later] - factor * cols[later][t : t + 1, :]
            rows = rows - factor * rows[t : t + 1, :]
        w[m, pl.ds(base, BLOCK), :] = rows
        left = jnp.where(lane >= base + BLOCK, rows[:, 0:n] * inverse, 0.0)
        w[m] = w[m] - dot(left, rows, 0, 0, HIGH)
        return carry

    lax.fori_loop(low, high, body, 0)


def identity(n):
    return (
        lax.broadcasted_iota(jnp.int32, (n, n), 0) == lax.broadcasted_iota(jnp.int32, (n, n), 1)
    ).astype(F32)


def load(w, m, a):
    n = w.shape[1]
    w[m, :, 0:n] = a
    w[m, :, n : 2 * n] = identity(n)


def factor_inverse(w, m):
    n = w.shape[1]
    diag = jnp.sum(w[m, :, 0:n] * identity(n), axis=1, keepdims=True)
    return w[m, :, n : 2 * n] * lax.rsqrt(diag)


def comm_kernel(
    devices, n_cells, n_sched,
    cell_ref, core_matrix_ref, rate_ref, well_ref, sched_ref, prof_ref,
    cells_ref, rows_ref, core_ref,
    *scratch,
):
    order = bit_order(devices)
    stages = len(order)
    recv = scratch[:stages]
    (
        ly, c_recv, c_acc, g_recv, g_acc, l_recv, l_acc, y_recv, y_acc, w, inv,
        x_ref, tile, mix, rates, k_ref, panel_t, gram_s,
        xs0, xr0, xs, xr, cs, cr, gs, gr, ls, lr, ys, yr,
    ) = scratch[stages:]
    cells, n = cell_ref.shape
    block = sched_ref.shape[1]
    wells, profiles = rate_ref.shape
    l_scale = PANEL_SCALE / n_cells
    me = lax.axis_index("cell")
    rows = x_ref.shape[1] // CHUNKS
    digits = [(me // (1 << b)) % 2 for b in order]
    partners = [me + (1 - 2 * d) * (1 << b) for d, b in zip(digits, order)]

    barrier = pltpu.get_barrier_semaphore()
    for p in partners:
        pl.semaphore_signal(
            barrier, inc=1, device_id={"cell": p}, device_id_type=pl.DeviceIdType.MESH
        )
    pl.semaphore_wait(barrier, stages)

    def remote(src, dst, ssem, rsem, s):
        return pltpu.make_async_remote_copy(
            src_ref=src, dst_ref=dst, send_sem=ssem, recv_sem=rsem,
            device_id={"cell": partners[s]}, device_id_type=pl.DeviceIdType.MESH,
        )

    def big(s, c):
        half = devices >> (s + 1)
        cur = x_ref if s == 0 else recv[s - 1]
        part = pl.ds(c * rows, rows)
        return remote(
            cur.at[pl.ds((1 - digits[s]) * half, half), part],
            recv[s].at[:, part], xs.at[s, c], xr.at[s, c], s,
        )

    def fold(s, c):
        half = devices >> (s + 1)
        cur = x_ref if s == 0 else recv[s - 1]
        part = pl.ds(c * rows, rows)
        if s == stages - 1:
            ly[part] = recv[s][0, part].astype(F32) + cur[digits[s], part].astype(F32)
        else:
            def body(i, carry):
                recv[s][i, part] = (
                    recv[s][i, part].astype(F32)
                    + cur[digits[s] * half + i, part].astype(F32)
                ).astype(BF16)
                return carry
            lax.fori_loop(0, half, body, 0)

    small = {"c": (c_recv, c_acc, cs, cr), "g": (g_recv, g_acc, gs, gr), "l": (l_recv, l_acc, ls, lr), "y": (y_recv, y_acc, ys, yr)}

    def hop(name, s):
        buf, acc, ssem, rsem = small[name]
        return remote(acc.at[s], buf.at[s], ssem.at[s], rsem.at[s], s)

    def begin(name, value):
        small[name][1][0] = value
        hop(name, 0).start()

    def advance(name, s):
        buf, acc, _, _ = small[name]
        hop(name, s).wait_recv()
        acc[s + 1] = acc[s] + buf[s]
        if s + 1 < stages:
            hop(name, s + 1).start()

    mix[...] = dot(cell_ref[...].astype(F32), core_matrix_ref[...], 1, 0, HIGH).astype(BF16)
    hot_well = (lax.broadcasted_iota(jnp.int32, (wells, cells), 0) == well_ref[...]).astype(F32)
    rates[...] = (TIME_STEP * dot(hot_well.T.astype(BF16), rate_ref[...], 1, 0)).astype(BF16)
    cell_t = cell_ref[...].astype(F32).T
    panel_t[0:n] = cell_t.astype(BF16)
    begin("c", dot(panel_t[0:n], cell_ref[...], 1, 0))
    k_ref[...] = jnp.zeros_like(k_ref)
    gram_s[...] = jnp.zeros_like(gram_s)

    def build(i, carry):
        sched = sched_ref[i]
        rebuilt = dot(mix[...], sched, 1, 1)
        hot = (
            lax.broadcasted_iota(jnp.int32, (profiles, block), 0) == prof_ref[i]
        ).astype(F32).astype(BF16)
        inject = dot(rates[...], hot, 1, 0)
        state = (
            rebuilt * ((1.0 + TIME_STEP) - TIME_STEP * (rebuilt * rebuilt)) + inject
        ).astype(BF16)
        tile[i] = state
        k_ref[...] += dot(state, sched, 1, 0)
        gram_s[...] += dot(sched.astype(F32).T.astype(BF16), sched, 1, 0)
        return carry

    for s in range(stages):
        lax.fori_loop(devices * s // stages, devices * (s + 1) // stages, build, 0)
        advance("c", s)

    k_ref[...] = k_ref[...] * (PANEL_SCALE / n_sched)
    k_t = k_ref[...].T
    panel_t[n : 2 * n] = k_t.astype(BF16)
    both = jnp.concatenate([cell_ref[...].astype(F32).T, k_t], axis=0)
    begin("g", dot(both, k_t, 1, 1, HIGH))

    half0 = devices // 2
    group = half0 // 2

    def project(i, carry):
        x_ref[i] = dot(panel_t[...], tile[owner_of(i, devices)], 1, 0).astype(BF16)
        return carry

    def first(i):
        return remote(
            x_ref.at[(1 - digits[0]) * half0 + i], recv[0].at[i], xs0.at[i], xr0.at[i], 0
        )

    for part in range(2):
        base = (1 - digits[0]) * half0 + part * group
        lax.fori_loop(base, base + group, project, 0)
        for i in range(part * group, (part + 1) * group):
            first(i).start()
    advance("g", 0)
    lax.fori_loop(digits[0] * half0, digits[0] * half0 + half0, project, 0)
    for i in range(half0):
        first(i).wait_recv()
    for c in range(CHUNKS):
        fold(0, c)
        big(1, c).start()
    advance("g", 1)

    pieces = n // BLOCK
    cut = pieces // 2
    g = lambda i: g_acc[stages, (i - 1) * n : i * n] if i else c_acc[stages]
    size_u = float(n_cells) ** 0.5
    size_v = float(n_sched) ** 0.5

    def schur(slot, corner, side, square):
        x = dot(inv[slot], side, 1, 0, HIGH)
        inv[slot + 1] = dot(x, inv[slot], 0, 0, HIGH)
        load(w, corner, square - dot(x, x, 0, 0, HIGH))

    def work_v_first():
        load(w, 1, gram_s[...])
        eliminate(w, 1, 0, cut)

    def work_v_second():
        eliminate(w, 1, cut, pieces)
        inv[3] = factor_inverse(w, 1)

    def work_u_first():
        load(w, 0, g(0))
        eliminate(w, 0, 0, pieces)
        inv[0] = factor_inverse(w, 0)

    def work_u_second():
        schur(0, 0, g(1), g(2))
        eliminate(w, 0, 0, cut)

    def work_u_third():
        eliminate(w, 0, cut, pieces)
        inv[2] = factor_inverse(w, 0)
        inv[1] = -dot(inv[2], inv[1], 1, 0, HIGH)

    def work_cells():
        cell = cell_ref[...].astype(F32)
        cells_ref[:, 0:n] = dot(cell, inv[0] * size_u, 1, 1, HIGH)
        cells_ref[:, n:] = dot(cell, inv[1] * size_u, 1, 1, HIGH) + dot(
            k_ref[...], inv[2] * size_u, 1, 1, HIGH
        )

    jobs = [work_v_first, work_v_second, work_u_first, work_u_second, work_u_third, work_cells]
    done = 0
    for d in range(stages + CHUNKS - 2):
        for s in range(stages - 1, 0, -1):
            c = d - s + 1
            if 0 <= c < CHUNKS:
                big(s, c).wait_recv()
                fold(s, c)
                if s + 1 < stages:
                    big(s + 1, c).start()
        if d + 2 < stages:
            advance("g", d + 2)
        if done < len(jobs) and d < stages + CHUNKS - 3 and (done < 3 or d + 3 >= stages):
            jobs[done]()
            done += 1

    left = ly[0:n]
    begin("l", dot(left, left, 1, 1, HIGH))
    begin("y", dot(ly[n : 2 * n], left, 1, 1, HIGH))
    for job in jobs[done : done + 1]:
        job()
    for s in range(stages):
        advance("l", s)
        for job in jobs[done + 1 + s : done + 2 + s]:
            job()
    ll = l_acc[stages] * (l_scale * l_scale)
    ck = g(1)
    schur(3, 1, ck.T * (n_sched / n_cells), ll)
    for s in range(stages):
        advance("y", s)
        eliminate(w, 1, pieces * s // stages, pieces * (s + 1) // stages)
    inv[5] = factor_inverse(w, 1)
    inv[4] = -dot(inv[5], inv[4], 1, 0, HIGH)
    yl = y_acc[stages] * l_scale
    u11, u21, u22, v11, v21, v22 = [inv[i] for i in range(6)]

    sched = sched_ref[me].astype(F32)
    l_rows = (left * l_scale).T
    rows_ref[:, 0:n] = dot(sched, v11 * size_v, 1, 1, HIGH)
    rows_ref[:, n:] = dot(sched, v21 * size_v, 1, 1, HIGH) + dot(
        l_rows, v22 * size_v, 1, 1, HIGH
    )

    k_unscale = n_sched / PANEL_SCALE
    m11 = ck * k_unscale
    m12 = ll * (1.0 / l_scale)
    m21 = g(2) * k_unscale
    t11 = dot(u11, m11, 1, 0, HIGH)
    t12 = dot(u11, m12, 1, 0, HIGH)
    t21 = dot(u21, m11, 1, 0, HIGH) + dot(u22, m21, 1, 0, HIGH)
    t22 = dot(u21, m12, 1, 0, HIGH) + dot(u22, yl, 1, 0, HIGH)
    scale = n / (float(n_cells) * float(n_sched)) ** 0.5
    core_ref[0:n, 0:n] = scale * dot(t11, v11, 1, 1, HIGH)
    core_ref[n:, 0:n] = scale * dot(t21, v11, 1, 1, HIGH)
    core_ref[0:n, n:] = scale * (dot(t11, v21, 1, 1, HIGH) + dot(t12, v22, 1, 1, HIGH))
    core_ref[n:, n:] = scale * (dot(t21, v21, 1, 1, HIGH) + dot(t22, v22, 1, 1, HIGH))
    for i in range(half0):
        first(i).wait_send()
    for s in range(stages):
        for c in range(CHUNKS):
            if s:
                big(s, c).wait_send()
        for name in small:
            hop(name, s).wait_send()


def local(cell_factor, sched_factor, core_matrix, rate_table, cell_well, sched_profile):
    cells, width = cell_factor.shape
    n_sched = sched_factor.shape[0]
    devices = lax.axis_size("cell")
    n_cells = cells * devices
    block = n_sched // devices
    wells, profiles = rate_table.shape
    stages = devices.bit_length() - 1
    sds = jax.ShapeDtypeStruct
    vmem = pl.BlockSpec(memory_space=pltpu.VMEM)
    dma = pltpu.SemaphoreType.DMA
    return pl.pallas_call(
        functools.partial(comm_kernel, devices, n_cells, n_sched),
        in_specs=[vmem] * 6,
        out_specs=[vmem] * 3,
        out_shape=[
            sds((cells, 2 * width), F32),
            sds((block, 2 * width), F32),
            sds((2 * width, 2 * width), F32),
        ],
        scratch_shapes=[
            pltpu.VMEM((devices >> (s + 1), 2 * width, block), BF16) for s in range(stages)
        ]
        + [
            pltpu.VMEM((2 * width, block), F32),
            pltpu.VMEM((stages, width, width), F32),
            pltpu.VMEM((stages + 1, width, width), F32),
            pltpu.VMEM((stages, 2 * width, width), F32),
            pltpu.VMEM((stages + 1, 2 * width, width), F32),
            pltpu.VMEM((stages, width, width), F32),
            pltpu.VMEM((stages + 1, width, width), F32),
            pltpu.VMEM((stages, width, width), F32),
            pltpu.VMEM((stages + 1, width, width), F32),
            pltpu.VMEM((2, width, 2 * width), F32),
            pltpu.VMEM((6, width, width), F32),
            pltpu.VMEM((devices, 2 * width, block), BF16),
            pltpu.VMEM((devices, cells, block), BF16),
            pltpu.VMEM((cells, width), BF16),
            pltpu.VMEM((cells, profiles), BF16),
            pltpu.VMEM((cells, width), F32),
            pltpu.VMEM((2 * width, cells), BF16),
            pltpu.VMEM((width, width), F32),
            dma((devices // 2,)), dma((devices // 2,)),
            dma((stages, CHUNKS)), dma((stages, CHUNKS)),
        ]
        + [dma((stages,))] * 8,
        compiler_params=pltpu.CompilerParams(
            collective_id=0, has_side_effects=True, vmem_limit_bytes=VMEM_LIMIT
        ),
    )(
        cell_factor, core_matrix, rate_table, cell_well.reshape(1, cells),
        sched_factor.reshape(devices, block, width),
        sched_profile.reshape(devices, 1, block),
    )


def solution(mesh):
    return jax.shard_map(
        local,
        mesh=mesh,
        in_specs=(
            P(("group", "cell"), None),
            P("group", None),
            P("group", None),
            P(),
            P(("group", "cell")),
            P("group"),
        ),
        out_specs=(P(("group", "cell"), None), P(("group", "cell"), None), P("group", None)),
        check_vma=False,
    )
```

```python
import functools

import jax
import jax.numpy as jnp
from jax import lax
from jax.experimental import pallas as pl
from jax.experimental.pallas import tpu as pltpu
from jax.sharding import PartitionSpec as P

TIME_STEP = 0.25
PANEL_SCALE = 8.0
HIGH = lax.Precision.HIGHEST
F32 = jnp.float32
BF16 = jnp.bfloat16
CHUNKS = 4
BLOCK = 16
VMEM_LIMIT = 64 * 1000 * 1000


def dot(a, b, ca, cb, precision=None):
    return lax.dot_general(
        a, b, (((ca,), (cb,)), ((), ())), precision=precision, preferred_element_type=F32
    )


def bit_order(devices):
    bits = devices.bit_length() - 1
    return list(range(bits))


def owner_of(place, devices):
    order = bit_order(devices)
    bits = len(order)
    total = 0
    for s, b in enumerate(order):
        total = total + ((place // (1 << (bits - 1 - s))) % 2) * (1 << b)
    return total


def eliminate(w, m, low, high):
    n = w.shape[1]
    lane = lax.broadcasted_iota(jnp.int32, (1, n), 1)
    rid = lax.broadcasted_iota(jnp.int32, (BLOCK, 1), 0)

    def body(b, carry):
        base = pl.multiple_of(b * BLOCK, BLOCK)
        rows = w[m, pl.ds(base, BLOCK), :]
        cols = [
            jnp.sum(jnp.where(lane == base + t, rows[:, 0:n], 0.0), axis=1, keepdims=True)
            for t in range(BLOCK)
        ]
        inverse = jnp.zeros((BLOCK, 1), F32)
        for t in range(BLOCK):
            recip = 1.0 / cols[t][t : t + 1, :]
            inverse = jnp.where(rid == t, recip, inverse)
            factor = jnp.where(rid > t, cols[t] * recip, 0.0)
            for later in range(t + 1, BLOCK):
                cols[later] = cols[later] - factor * cols[later][t : t + 1, :]
            rows = rows - factor * rows[t : t + 1, :]
        w[m, pl.ds(base, BLOCK), :] = rows
        left = jnp.where(lane >= base + BLOCK, rows[:, 0:n] * inverse, 0.0)
        w[m] = w[m] - dot(left, rows, 0, 0, HIGH)
        return carry

    lax.fori_loop(low, high, body, 0)


def identity(n):
    return (
        lax.broadcasted_iota(jnp.int32, (n, n), 0) == lax.broadcasted_iota(jnp.int32, (n, n), 1)
    ).astype(F32)


def load(w, m, a):
    n = w.shape[1]
    w[m, :, 0:n] = a
    w[m, :, n : 2 * n] = identity(n)


def factor_inverse(w, m):
    n = w.shape[1]
    diag = jnp.sum(w[m, :, 0:n] * identity(n), axis=1, keepdims=True)
    return w[m, :, n : 2 * n] * lax.rsqrt(diag)


def comm_kernel(
    devices, n_cells, n_sched,
    cell_ref, core_matrix_ref, rate_ref, well_ref, sched_ref, prof_ref,
    cells_ref, rows_ref, core_ref,
    *scratch,
):
    order = bit_order(devices)
    stages = len(order)
    recv = scratch[:stages]
    (
        ly, c_recv, c_acc, g_recv, g_acc, l_recv, l_acc, y_recv, y_acc, w, inv,
        x_ref, tile, mix, rates, k_ref, panel_t, gram_s,
        xs0, xr0, xs, xr, cs, cr, gs, gr, ls, lr, ys, yr,
    ) = scratch[stages:]
    cells, n = cell_ref.shape
    block = sched_ref.shape[1]
    wells, profiles = rate_ref.shape
    l_scale = PANEL_SCALE / n_cells
    me = lax.axis_index("cell")
    rows = x_ref.shape[1] // CHUNKS
    digits = [(me // (1 << b)) % 2 for b in order]
    partners = [me + (1 - 2 * d) * (1 << b) for d, b in zip(digits, order)]

    barrier = pltpu.get_barrier_semaphore()
    for p in partners:
        pl.semaphore_signal(
            barrier, inc=1, device_id={"cell": p}, device_id_type=pl.DeviceIdType.MESH
        )
    pl.semaphore_wait(barrier, stages)

    def remote(src, dst, ssem, rsem, s):
        return pltpu.make_async_remote_copy(
            src_ref=src, dst_ref=dst, send_sem=ssem, recv_sem=rsem,
            device_id={"cell": partners[s]}, device_id_type=pl.DeviceIdType.MESH,
        )

    def big(s, c):
        half = devices >> (s + 1)
        cur = x_ref if s == 0 else recv[s - 1]
        part = pl.ds(c * rows, rows)
        return remote(
            cur.at[pl.ds((1 - digits[s]) * half, half), part],
            recv[s].at[:, part], xs.at[s, c], xr.at[s, c], s,
        )

    def fold(s, c):
        half = devices >> (s + 1)
        cur = x_ref if s == 0 else recv[s - 1]
        part = pl.ds(c * rows, rows)
        if s == stages - 1:
            ly[part] = recv[s][0, part].astype(F32) + cur[digits[s], part].astype(F32)
        else:
            def body(i, carry):
                recv[s][i, part] = (
                    recv[s][i, part].astype(F32)
                    + cur[digits[s] * half + i, part].astype(F32)
                ).astype(BF16)
                return carry
            lax.fori_loop(0, half, body, 0)

    small = {"c": (c_recv, c_acc, cs, cr), "g": (g_recv, g_acc, gs, gr), "l": (l_recv, l_acc, ls, lr), "y": (y_recv, y_acc, ys, yr)}

    def hop(name, s):
        buf, acc, ssem, rsem = small[name]
        return remote(acc.at[s], buf.at[s], ssem.at[s], rsem.at[s], s)

    def begin(name, value):
        small[name][1][0] = value
        hop(name, 0).start()

    def advance(name, s):
        buf, acc, _, _ = small[name]
        hop(name, s).wait_recv()
        acc[s + 1] = acc[s] + buf[s]
        if s + 1 < stages:
            hop(name, s + 1).start()

    mix[...] = dot(cell_ref[...].astype(F32), core_matrix_ref[...], 1, 0, HIGH).astype(BF16)
    hot_well = (lax.broadcasted_iota(jnp.int32, (wells, cells), 0) == well_ref[...]).astype(F32)
    rates[...] = (TIME_STEP * dot(hot_well.T.astype(BF16), rate_ref[...], 1, 0)).astype(BF16)
    cell_t = cell_ref[...].astype(F32).T
    panel_t[0:n] = cell_t.astype(BF16)
    begin("c", dot(panel_t[0:n], cell_ref[...], 1, 0))
    k_ref[...] = jnp.zeros_like(k_ref)
    gram_s[...] = jnp.zeros_like(gram_s)

    def build(i, carry):
        sched = sched_ref[i]
        rebuilt = dot(mix[...], sched, 1, 1)
        hot = (
            lax.broadcasted_iota(jnp.int32, (profiles, block), 0) == prof_ref[i]
        ).astype(F32).astype(BF16)
        inject = dot(rates[...], hot, 1, 0)
        state = (
            rebuilt * ((1.0 + TIME_STEP) - TIME_STEP * (rebuilt * rebuilt)) + inject
        ).astype(BF16)
        tile[i] = state
        k_ref[...] += dot(state, sched, 1, 0)
        gram_s[...] += dot(sched.astype(F32).T.astype(BF16), sched, 1, 0)
        return carry

    for s in range(stages):
        lax.fori_loop(devices * s // stages, devices * (s + 1) // stages, build, 0)
        advance("c", s)

    k_ref[...] = k_ref[...] * (PANEL_SCALE / n_sched)
    k_t = k_ref[...].T
    panel_t[n : 2 * n] = k_t.astype(BF16)
    both = jnp.concatenate([cell_ref[...].astype(F32).T, k_t], axis=0)
    begin("g", dot(both, k_t, 1, 1, HIGH))

    half0 = devices // 2
    group = half0 // 2

    def project(i, carry):
        x_ref[i] = dot(panel_t[...], tile[owner_of(i, devices)], 1, 0).astype(BF16)
        return carry

    def first(i):
        return remote(
            x_ref.at[(1 - digits[0]) * half0 + i], recv[0].at[i], xs0.at[i], xr0.at[i], 0
        )

    for part in range(2):
        base = (1 - digits[0]) * half0 + part * group
        lax.fori_loop(base, base + group, project, 0)
        for i in range(part * group, (part + 1) * group):
            first(i).start()
    advance("g", 0)
    lax.fori_loop(digits[0] * half0, digits[0] * half0 + half0, project, 0)
    for i in range(half0):
        first(i).wait_recv()
    for c in range(CHUNKS):
        fold(0, c)
        big(1, c).start()
    advance("g", 1)

    pieces = n // BLOCK
    cut = pieces // 2
    g = lambda i: g_acc[stages, (i - 1) * n : i * n] if i else c_acc[stages]
    size_u = float(n_cells) ** 0.5
    size_v = float(n_sched) ** 0.5

    def schur(slot, corner, side, square):
        x = dot(inv[slot], side, 1, 0, HIGH)
        inv[slot + 1] = dot(x, inv[slot], 0, 0, HIGH)
        load(w, corner, square - dot(x, x, 0, 0, HIGH))

    def work_v_first():
        load(w, 1, gram_s[...])
        eliminate(w, 1, 0, cut)

    def work_v_second():
        eliminate(w, 1, cut, pieces)
        inv[3] = factor_inverse(w, 1)

    def work_u_first():
        load(w, 0, g(0))
        eliminate(w, 0, 0, pieces)
        inv[0] = factor_inverse(w, 0)

    def work_u_second():
        schur(0, 0, g(1), g(2))
        eliminate(w, 0, 0, cut)

    def work_u_third():
        eliminate(w, 0, cut, pieces)
        inv[2] = factor_inverse(w, 0)
        inv[1] = -dot(inv[2], inv[1], 1, 0, HIGH)

    def work_cells():
        cell = cell_ref[...].astype(F32)
        cells_ref[:, 0:n] = dot(cell, inv[0] * size_u, 1, 1, HIGH)
        cells_ref[:, n:] = dot(cell, inv[1] * size_u, 1, 1, HIGH) + dot(
            k_ref[...], inv[2] * size_u, 1, 1, HIGH
        )

    jobs = [work_v_first, work_v_second, work_u_first, work_u_second, work_u_third, work_cells]
    done = 0
    for d in range(stages + CHUNKS - 2):
        for s in range(stages - 1, 0, -1):
            c = d - s + 1
            if 0 <= c < CHUNKS:
                big(s, c).wait_recv()
                fold(s, c)
                if s + 1 < stages:
                    big(s + 1, c).start()
        if d + 2 < stages:
            advance("g", d + 2)
        if done < len(jobs) and d < stages + CHUNKS - 3 and (done < 3 or d + 3 >= stages):
            jobs[done]()
            done += 1

    left = ly[0:n]
    begin("l", dot(left, left, 1, 1, HIGH))
    begin("y", dot(ly[n : 2 * n], left, 1, 1, HIGH))
    for job in jobs[done : done + 1]:
        job()
    for s in range(stages):
        advance("l", s)
        for job in jobs[done + 1 + s : done + 2 + s]:
            job()
    ll = l_acc[stages] * (l_scale * l_scale)
    ck = g(1)
    schur(3, 1, ck.T * (n_sched / n_cells), ll)
    for s in range(stages):
        advance("y", s)
        eliminate(w, 1, pieces * s // stages, pieces * (s + 1) // stages)
    inv[5] = factor_inverse(w, 1)
    inv[4] = -dot(inv[5], inv[4], 1, 0, HIGH)
    yl = y_acc[stages] * l_scale
    u11, u21, u22, v11, v21, v22 = [inv[i] for i in range(6)]

    sched = sched_ref[me].astype(F32)
    l_rows = (left * l_scale).T
    rows_ref[:, 0:n] = dot(sched, v11 * size_v, 1, 1, HIGH)
    rows_ref[:, n:] = dot(sched, v21 * size_v, 1, 1, HIGH) + dot(
        l_rows, v22 * size_v, 1, 1, HIGH
    )

    k_unscale = n_sched / PANEL_SCALE
    m11 = ck * k_unscale
    m12 = ll * (1.0 / l_scale)
    m21 = g(2) * k_unscale
    t11 = dot(u11, m11, 1, 0, HIGH)
    t12 = dot(u11, m12, 1, 0, HIGH)
    t21 = dot(u21, m11, 1, 0, HIGH) + dot(u22, m21, 1, 0, HIGH)
    t22 = dot(u21, m12, 1, 0, HIGH) + dot(u22, yl, 1, 0, HIGH)
    scale = n / (float(n_cells) * float(n_sched)) ** 0.5
    core_ref[0:n, 0:n] = scale * dot(t11, v11, 1, 1, HIGH)
    core_ref[n:, 0:n] = scale * dot(t21, v11, 1, 1, HIGH)
    core_ref[0:n, n:] = scale * (dot(t11, v21, 1, 1, HIGH) + dot(t12, v22, 1, 1, HIGH))
    core_ref[n:, n:] = scale * (dot(t21, v21, 1, 1, HIGH) + dot(t22, v22, 1, 1, HIGH))
    for i in range(half0):
        first(i).wait_send()
    for s in range(stages):
        for c in range(CHUNKS):
            if s:
                big(s, c).wait_send()
        for name in small:
            hop(name, s).wait_send()


def hand_on(*refs):
    half = len(refs) // 2
    for source, target in zip(refs[:half], refs[half:]):
        target[...] = source[...]


def local(cell_factor, sched_factor, core_matrix, rate_table, cell_well, sched_profile):
    cells, width = cell_factor.shape
    n_sched = sched_factor.shape[0]
    devices = lax.axis_size("cell")
    n_cells = cells * devices
    block = n_sched // devices
    wells, profiles = rate_table.shape
    stages = devices.bit_length() - 1
    sds = jax.ShapeDtypeStruct
    vmem = pl.BlockSpec(memory_space=pltpu.VMEM)
    dma = pltpu.SemaphoreType.DMA
    outs = pl.pallas_call(
        functools.partial(comm_kernel, devices, n_cells, n_sched),
        in_specs=[vmem] * 6,
        out_specs=[vmem] * 3,
        out_shape=[
            sds((cells, 2 * width), F32),
            sds((block, 2 * width), F32),
            sds((2 * width, 2 * width), F32),
        ],
        scratch_shapes=[
            pltpu.VMEM((devices >> (s + 1), 2 * width, block), BF16) for s in range(stages)
        ]
        + [
            pltpu.VMEM((2 * width, block), F32),
            pltpu.VMEM((stages, width, width), F32),
            pltpu.VMEM((stages + 1, width, width), F32),
            pltpu.VMEM((stages, 2 * width, width), F32),
            pltpu.VMEM((stages + 1, 2 * width, width), F32),
            pltpu.VMEM((stages, width, width), F32),
            pltpu.VMEM((stages + 1, width, width), F32),
            pltpu.VMEM((stages, width, width), F32),
            pltpu.VMEM((stages + 1, width, width), F32),
            pltpu.VMEM((2, width, 2 * width), F32),
            pltpu.VMEM((6, width, width), F32),
            pltpu.VMEM((devices, 2 * width, block), BF16),
            pltpu.VMEM((devices, cells, block), BF16),
            pltpu.VMEM((cells, width), BF16),
            pltpu.VMEM((cells, profiles), BF16),
            pltpu.VMEM((cells, width), F32),
            pltpu.VMEM((2 * width, cells), BF16),
            pltpu.VMEM((width, width), F32),
            dma((devices // 2,)), dma((devices // 2,)),
            dma((stages, CHUNKS)), dma((stages, CHUNKS)),
        ]
        + [dma((stages,))] * 8,
        compiler_params=pltpu.CompilerParams(
            collective_id=0, has_side_effects=True, vmem_limit_bytes=VMEM_LIMIT
        ),
    )(
        cell_factor, core_matrix, rate_table, cell_well.reshape(1, cells),
        sched_factor.reshape(devices, block, width),
        sched_profile.reshape(devices, 1, block),
    )
    return tuple(
        pl.pallas_call(
            hand_on,
            in_specs=[vmem] * 3,
            out_specs=[vmem] * 3,
            out_shape=[sds(o.shape, o.dtype) for o in outs],
        )(*outs)
    )


def solution(mesh):
    return jax.shard_map(
        local,
        mesh=mesh,
        in_specs=(
            P(("group", "cell"), None),
            P("group", None),
            P("group", None),
            P(),
            P(("group", "cell")),
            P("group"),
        ),
        out_specs=(P(("group", "cell"), None), P(("group", "cell"), None), P("group", None)),
        check_vma=False,
    )
```
